32 devices in a mesh: row: 8 (over y, x, core), col: 4 (over z).
Axes of the slice: x: 2, y: 2, z: 4, core: 2. Of those that a mesh axis runs over, the one named last changes fastest.
Arguments:
- gate_input: bfloat16 [1024, 28672], P('row', 'col'), may hold values from -6 to 6
- up_input: bfloat16 [1024, 28672], P('row', 'col'), may hold values from -6 to 6
- grad_output: bfloat16 [1024, 8192], P('col', 'row'), may hold values from -0.75 to 0.75
- down_weight: bfloat16 [28672, 8192], P('col', 'row'), may hold values from -0.0625 to 0.0625
Outputs:
- grad_gate: bfloat16 [1024, 28672], P('row', 'col')
- grad_up: bfloat16 [1024, 28672], P('row', 'col')
- grad_weight: float32 [28672, 8192], P('col', 'row')
The draws below stay inside these ranges and needn't reach their ends.
All inputs are finite; a program needn't handle non-finite values.
Results may differ from the reference program's by a relative error of at most 0.013.
Values may be sent and summed in bfloat16 or wider, within the bound.
A program may use at most 192 MiB of HBM per device.

```python
import jax
import jax.numpy as jnp
from jax import lax

D = 8192
FF = 28672
TOKENS = 1024
N_ROW = 8


def strengthened(array, key, source, target, shards_of, factor):
    owner, partner = [(jnp.arange(array.shape[position]) // (array.shape[position] // shards_of)).reshape([-1 if axis == position else 1 for axis in range(array.ndim)]) for position in (source, target)]
    chosen = jax.random.permutation(key, shards_of)[partner]
    strong = (owner == chosen) | (owner == (partner + shards_of // 2) % shards_of)
    return jnp.where(strong, factor * array, array)


def block_scale(rng, dims, shards, smallest, high):
    def one(axis_at, shards_of):
        steps = jax.random.uniform(jax.random.fold_in(jax.random.fold_in(rng, 6), axis_at), (shards_of,), jnp.float32, smallest / len(shards), high / len(shards))
        return jnp.repeat(jnp.exp(steps), dims[axis_at] // shards_of).reshape((-1,) + (1,) * (len(dims) - axis_at - 1))

    level = one(*shards[0])
    for cut in shards[1:]:
        level = level * one(*cut)
    return level


def normal_values(rng, shape, spread, bound, split=(), kind=jnp.bfloat16):
    entries = jax.random.normal(rng, shape, jnp.float32) * spread
    if len(split) > 0:
        entries = block_scale(rng, shape, split, -0.22, 0.18) * entries
    return jnp.clip(entries, min=-bound, max=bound).astype(kind)


def gaussian_with(stream_key, shape, deviation, reach, split, heavy, kind=jnp.bfloat16):
    drawn = deviation * jax.random.normal(stream_key, shape, jnp.float32)
    if split:
        drawn = drawn * block_scale(stream_key, shape, split, -0.22, 0.18)
    return jnp.clip(strengthened(drawn, jax.random.fold_in(stream_key, 3), *heavy), -reach, reach).astype(kind)


def setup_inputs(seed: int = 0) -> dict:
    streams_of = jax.random.split(jax.random.key(seed), 5)
    return {
        "gate_input": normal_values(streams_of[0], (TOKENS, FF), 1.0, 6.0, ((0, 8), (1, 4))),
        "up_input": normal_values(streams_of[1], (TOKENS, FF), 1.0, 6.0, ((0, 8), (1, 4))),
        "grad_output": gaussian_with(streams_of[2], (TOKENS, D), (4.0 / TOKENS ** 0.5), 0.75, ((0, 4), (1, 8)), (1, 0, 8, 2.0)),
        "down_weight": normal_values(streams_of[3], (FF, D), D ** -0.5, 0.0625, ((0, 4), (1, 8))),
    }


def reference(gate_input, up_input, grad_output, down_weight):
    gate_value = gate_input.astype(jnp.float32)
    up_value = up_input.astype(jnp.float32)
    sigma = jax.nn.sigmoid(gate_value)
    swish = gate_value * sigma
    hidden = (swish * up_value).astype(jnp.bfloat16)
    width_block = D // N_ROW
    grad_hidden = jnp.zeros((TOKENS, FF), jnp.float32)
    for block_index in range(N_ROW):
        low = block_index * width_block
        partial_sum = jnp.dot(grad_output[:, low:low + width_block], down_weight[:, low:low + width_block].T, preferred_element_type=jnp.float32)
        rounded = lax.optimization_barrier(partial_sum.astype(jnp.bfloat16))
        grad_hidden = grad_hidden + rounded.astype(jnp.float32)
    grad_up = (grad_hidden * swish).astype(jnp.bfloat16)
    grad_gate = (grad_hidden * up_value * sigma * (1.0 + gate_value * (1.0 - sigma))).astype(jnp.bfloat16)
    grad_weight = jnp.dot(hidden.T, grad_output, preferred_element_type=jnp.float32)
    return grad_gate, grad_up, grad_weight
```

```python
import functools

import jax
import jax.numpy as jnp
from jax import lax
from jax.experimental import pallas as pl
from jax.experimental.pallas import tpu as pltpu
from jax.sharding import PartitionSpec as P

F32 = jnp.float32
BF16 = jnp.bfloat16
MESH = pl.DeviceIdType.MESH


def snake(place):
    return (place // 2) * 2 + (place + place // 2) % 2


def tile_of(width):
    return 256 if width % 256 == 0 else 128


def exchange_kernel(
    n_row, n_col, gate_ref, up_ref, go_ref, w_ref,
    hid_ref, gath_ref, gh_ref,
    hid_v, w_v, go_v, part, rs_out, rs_in, sib_out, sib_in,
    ag_ss, ag_rs, push_ss, push_rs, z_ss, z_rs, gos_ss, gos_rs, w_ss, w_rs, rs_ss, rs_rs,
    fin_ss, fin_rs, loc,
):
    me, z = lax.axis_index("row"), lax.axis_index("col")
    core, chip = me % 2, me // 2
    n = n_row // 2
    place = snake(chip)
    tok, ff = gate_ref.shape
    rows = go_ref.shape[0]
    half, quarter = ff // 2, ff // 4
    tile = tile_of(quarter)

    def row_of(ring_place):
        return snake(ring_place) * 2 + core

    sibling = (chip * 2 + 1 - core, z)
    ahead = (row_of((place + 1) % n), z)
    behind = (row_of((place + n - 1) % n), z)
    towards = (ahead, behind)
    z_peers = [(me, (z + step) % n_col) for step in range(1, n_col)]

    barrier = pltpu.get_barrier_semaphore()
    for peer in [ahead, behind, sibling] + z_peers:
        pl.semaphore_signal(barrier, inc=1, device_id=peer, device_id_type=MESH)
    pl.semaphore_wait(barrier, 3 + len(z_peers))

    sent = []

    def remote(src, dst, ss, rs, peer):
        copy = pltpu.make_async_remote_copy(
            src_ref=src, dst_ref=dst, send_sem=ss, recv_sem=rs, device_id=peer, device_id_type=MESH
        )
        copy.start()
        sent.append(copy)
        return copy

    go_here = go_v.at[core, pl.ds(z * rows, rows)]
    z_in = []
    for step, peer in enumerate(z_peers):
        z_in.append(remote(go_ref, go_here, z_ss.at[step], z_rs.at[step], peer))

    ag_in, push_in = {}, []

    def push(src_row, d, k, slot, src=None):
        span = pl.ds((2 * d + k) * quarter, quarter)
        dst = hid_ref.at[src_row, span]
        push_in.append(
            remote(dst if src is None else src, dst, push_ss.at[d, k, slot], push_rs.at[d, k, slot], sibling)
        )

    for k in range(2):
        for d in range(2):
            first = (2 * d + k) * quarter

            @pl.loop(0, quarter // tile)
            def _(j):
                span = pl.ds(pl.multiple_of(first + j * tile, 128), tile)
                gate = gate_ref[:, span].astype(F32)
                value = gate * jax.nn.sigmoid(gate) * up_ref[:, span].astype(F32)
                hid_v[span, :] = value.T.astype(BF16)

            src = hid_v.at[pl.ds(first, quarter)]
            ag_in[d, k] = remote(
                src, hid_ref.at[me, pl.ds(first, quarter)], ag_ss.at[d, k, 0], ag_rs.at[d, k, 0], towards[d]
            )

    own_go = pltpu.make_async_copy(go_ref, go_here, loc.at[0])
    own_go.start()
    go_in = [remote(go_ref, go_here, gos_ss.at[0], gos_rs.at[0], sibling)]
    w_in = remote(
        w_ref.at[pl.ds((1 - core) * half, half)], w_v.at[core], w_ss.at[0], w_rs.at[0], sibling
    )
    own_w = pltpu.make_async_copy(w_ref.at[pl.ds(core * half, half)], w_v.at[core], loc.at[1])
    own_w.start()
    for k in range(2):
        for d in range(2):
            push(me, d, k, 0, hid_v.at[pl.ds((2 * d + k) * quarter, quarter)])
    own_hid = pltpu.make_async_copy(hid_v, hid_ref.at[me], loc.at[2])
    own_hid.start()

    def arrived(step, d, k):
        ag_in[d, k].wait_recv()
        origin = (place + n - step - 1) % n if d == 0 else (place + step + 1) % n
        src_row = row_of(origin)
        if step < n - 2:
            block = hid_ref.at[src_row, pl.ds((2 * d + k) * quarter, quarter)]
            ag_in[d, k] = remote(
                block, block, ag_ss.at[d, k, step + 1], ag_rs.at[d, k, step + 1], towards[d]
            )
        push(src_row, d, k, step + 1)

    for step in range(n - 2):
        for k in range(2):
            for d in range(2):
                arrived(step, d, k)

    for step in range(n_col - 1):
        z_in[step].wait_recv()
        block = go_v.at[core, pl.ds((z + n_col - step - 1) % n_col * rows, rows)]
        go_in.append(remote(block, block, gos_ss.at[step + 1], gos_rs.at[step + 1], sibling))
    own_go.wait()
    out_go = pltpu.make_async_copy(go_v.at[core], gath_ref, loc.at[3])
    out_go.start()
    for copy in go_in:
        copy.wait_recv()
    w_in.wait_recv()
    own_w.wait()

    def partial_of(ring_place, d):
        base = pl.multiple_of(snake(ring_place) * (2 * tok), 2 * tok)

        @pl.loop(0, quarter // tile)
        def _(j):
            columns = pl.ds(pl.multiple_of(d * quarter + j * tile, 128), tile)
            total = None
            for c in range(2):
                term = lax.dot_general(
                    go_v[c, pl.ds(base, 2 * tok), :], w_v[c, columns, :],
                    (((1,), (1,)), ((), ())), preferred_element_type=F32,
                )
                total = term if total is None else total + term
            part[d, :, pl.ds(pl.multiple_of(j * tile, 128), tile)] = total

    offsets = (pl.multiple_of((1 - core) * tok, tok), pl.multiple_of(core * tok, tok))
    rs_hop = {}
    for step in range(n - 1):
        for d in range(2):
            partial_of((place + n - 1 - step) % n if d == 0 else (place + 1 + step) % n, d)
        for k in range(2):
            for d in range(2):
                if step > 0:
                    rs_hop[d, k].wait_recv()

                @pl.loop(0, quarter // tile)
                def _(j):
                    span = pl.ds(pl.multiple_of(j * tile, 128), tile)
                    value = part[d, pl.ds(offsets[k], tok), span]
                    if step > 0:
                        value = value + rs_in[d, k, step - 1, :, span].astype(F32)
                    rs_out[d, k, step, :, span] = value.astype(BF16)

                rs_hop[d, k] = remote(
                    rs_out.at[d, k, step], rs_in.at[d, k, step],
                    rs_ss.at[d, k, step], rs_rs.at[d, k, step], towards[d],
                )
        if step == 0:
            for k in range(2):
                for d in range(2):
                    arrived(n - 2, d, k)

    for d in range(2):
        partial_of(place, d)
    fin = []
    for k in range(2):
        for d in range(2):
            rs_hop[d, k].wait_recv()

            @pl.loop(0, quarter // tile)
            def _(j):
                span = pl.ds(pl.multiple_of(j * tile, 128), tile)
                value = part[d, pl.ds(offsets[k], tok), span] + rs_in[d, k, n - 2, :, span].astype(F32)
                if k == 0:
                    sib_out[d, :, span] = value.astype(BF16)
                else:
                    gh_ref[:, pl.ds(pl.multiple_of(core * half + d * quarter + j * tile, 128), tile)] = value

            if k == 0:
                fin.append(remote(sib_out.at[d], sib_in.at[d], fin_ss.at[d], fin_rs.at[d], sibling))
    for d in range(2):
        fin[d].wait_recv()

        @pl.loop(0, quarter // tile)
        def _(j):
            span = pl.ds(pl.multiple_of(j * tile, 128), tile)
            columns = pl.ds(pl.multiple_of((1 - core) * half + d * quarter + j * tile, 128), tile)
            gh_ref[:, columns] = sib_in[d, :, span].astype(F32)

    for copy in push_in:
        copy.wait_recv()
    for copy in sent:
        copy.wait_send()
    own_hid.wait()
    out_go.wait()


def exchange(n_row, n_col, gate, up, go, w):
    tok, ff = gate.shape
    rows, width = go.shape
    n = n_row // 2
    quarter = ff // 4
    dma = pltpu.SemaphoreType.DMA
    whole = pl.BlockSpec(memory_space=pltpu.VMEM)
    hbm = pl.BlockSpec(memory_space=pl.ANY)
    return pl.pallas_call(
        functools.partial(exchange_kernel, n_row, n_col),
        out_shape=(
            jax.ShapeDtypeStruct((n_row, ff, tok), BF16),
            jax.ShapeDtypeStruct((n_col * rows, width), BF16),
            jax.ShapeDtypeStruct((tok, ff), F32),
        ),
        in_specs=[whole, whole, hbm, hbm],
        out_specs=(hbm, hbm, whole),
        scratch_shapes=[
            pltpu.VMEM((ff, tok), BF16),
            pltpu.VMEM((2, ff // 2, width), BF16),
            pltpu.VMEM((2, n_col * rows, width), BF16),
            pltpu.VMEM((2, 2 * tok, quarter), F32),
            pltpu.VMEM((2, 2, n - 1, tok, quarter), BF16),
            pltpu.VMEM((2, 2, n - 1, tok, quarter), BF16),
            pltpu.VMEM((2, tok, quarter), BF16),
            pltpu.VMEM((2, tok, quarter), BF16),
            dma((2, 2, n - 1)),
            dma((2, 2, n - 1)),
            dma((2, 2, n)),
            dma((2, 2, n)),
            dma((n_col - 1,)),
            dma((n_col - 1,)),
            dma((n_col,)),
            dma((n_col,)),
            dma((1,)),
            dma((1,)),
            dma((2, 2, n - 1)),
            dma((2, 2, n - 1)),
            dma((2,)),
            dma((2,)),
            dma((4,)),
        ],
        compiler_params=pltpu.CompilerParams(
            collective_id=0, has_side_effects=True, vmem_limit_bytes=56 * 2**20
        ),
    )(gate, up, go, w)


def finish_kernel(n_row, hid_ref, go_ref, gate_ref, up_ref, gh_ref, gg_ref, gu_ref, gw_ref):
    lhs = jnp.concatenate([hid_ref[r] for r in range(n_row)], axis=1)
    gw_ref[...] = jnp.dot(lhs, go_ref[...], preferred_element_type=F32)
    gate = gate_ref[...].astype(F32)
    grad_hidden = gh_ref[...]
    sigma = jax.nn.sigmoid(gate)
    gu_ref[...] = (grad_hidden * (gate * sigma)).astype(BF16)
    gg_ref[...] = (
        grad_hidden * up_ref[...].astype(F32) * sigma * (1.0 + gate * (1.0 - sigma))
    ).astype(BF16)


def finish(hid, go, gate, up, gh):
    n_row, ff, tok = hid.shape
    tokens, width = go.shape
    tile = 512 if ff % 512 == 0 else 256
    strip = pl.BlockSpec((tok, tile), lambda j: (0, j))
    return pl.pallas_call(
        functools.partial(finish_kernel, n_row),
        grid=(ff // tile,),
        out_shape=(
            jax.ShapeDtypeStruct((tok, ff), BF16),
            jax.ShapeDtypeStruct((tok, ff), BF16),
            jax.ShapeDtypeStruct((ff, width), F32),
        ),
        in_specs=[
            pl.BlockSpec((n_row, tile, tok), lambda j: (0, j, 0)),
            pl.BlockSpec((tokens, width), lambda j: (0, 0)),
            strip, strip, strip,
        ],
        out_specs=(strip, strip, pl.BlockSpec((tile, width), lambda j: (j, 0))),
        compiler_params=pltpu.CompilerParams(vmem_limit_bytes=48 * 2**20),
    )(hid, go, gate, up, gh)


def solution(mesh):
    n_row, n_col = mesh.shape["row"], mesh.shape["col"]

    def body(gate_input, up_input, grad_output, down_weight):
        hid, go, gh = exchange(n_row, n_col, gate_input, up_input, grad_output, down_weight)
        return finish(hid, go, gate_input, up_input, gh)

    placed = (P("row", "col"), P("row", "col"), P("col", "row"), P("col", "row"))
    return jax.shard_map(
        body,
        mesh=mesh,
        in_specs=placed,
        out_specs=(P("row", "col"), P("row", "col"), P("col", "row")),
        check_vma=False,
    )
```

```python
import functools

import jax
import jax.numpy as jnp
from jax import lax
from jax.experimental import pallas as pl
from jax.experimental.pallas import tpu as pltpu
from jax.sharding import PartitionSpec as P

F32 = jnp.float32
BF16 = jnp.bfloat16
MESH = pl.DeviceIdType.MESH


def snake(place):
    return (place // 2) * 2 + (place + place // 2) % 2


def tile_of(width):
    return 256 if width % 256 == 0 else 128


def exchange_kernel(
    n_row, n_col, gate_ref, up_ref, go_ref, w_ref,
    hid_ref, gath_ref, own_ref, last_ref0, last_ref1, last_ref2, last_ref3,
    hid_v, w_v, go_v, part, own_v, rs_out, rs_in, sib_out, sib_in,
    ag_ss, ag_rs, push_ss, push_rs, z_ss, z_rs, gos_ss, gos_rs, w_ss, w_rs, rs_ss, rs_rs,
    fin_ss, fin_rs, loc, last_sem,
):
    me, z = lax.axis_index("row"), lax.axis_index("col")
    core, chip = me % 2, me // 2
    n = n_row // 2
    place = snake(chip)
    tok, ff = gate_ref.shape
    rows = go_ref.shape[0]
    half, quarter = ff // 2, ff // 4
    tile = tile_of(quarter)

    def row_of(ring_place):
        return snake(ring_place) * 2 + core

    sibling = (chip * 2 + 1 - core, z)
    ahead = (row_of((place + 1) % n), z)
    behind = (row_of((place + n - 1) % n), z)
    towards = (ahead, behind)
    z_peers = [(me, (z + step) % n_col) for step in range(1, n_col)]

    barrier = pltpu.get_barrier_semaphore()
    for peer in [ahead, behind, sibling] + z_peers:
        pl.semaphore_signal(barrier, inc=1, device_id=peer, device_id_type=MESH)
    pl.semaphore_wait(barrier, 3 + len(z_peers))

    sent = []

    def remote(src, dst, ss, rs, peer):
        copy = pltpu.make_async_remote_copy(
            src_ref=src, dst_ref=dst, send_sem=ss, recv_sem=rs, device_id=peer, device_id_type=MESH
        )
        copy.start()
        sent.append(copy)
        return copy

    go_here = go_v.at[core, pl.ds(z * rows, rows)]
    z_in = []
    for step, peer in enumerate(z_peers):
        z_in.append(remote(go_ref, go_here, z_ss.at[step], z_rs.at[step], peer))

    ag_in, push_in = {}, []

    def push(src_row, d, k, slot, src=None):
        span = pl.ds((2 * d + k) * quarter, quarter)
        dst = hid_ref.at[src_row, span]
        push_in.append(
            remote(dst if src is None else src, dst, push_ss.at[d, k, slot], push_rs.at[d, k, slot], sibling)
        )

    for k in range(2):
        for d in range(2):
            first = (2 * d + k) * quarter

            @pl.loop(0, quarter // tile)
            def _(j):
                span = pl.ds(pl.multiple_of(first + j * tile, 128), tile)
                gate = gate_ref[:, span].astype(F32)
                value = gate * jax.nn.sigmoid(gate) * up_ref[:, span].astype(F32)
                hid_v[span, :] = value.T.astype(BF16)

            src = hid_v.at[pl.ds(first, quarter)]
            ag_in[d, k] = remote(
                src, hid_ref.at[me, pl.ds(first, quarter)], ag_ss.at[d, k, 0], ag_rs.at[d, k, 0], towards[d]
            )

    own_go = pltpu.make_async_copy(go_ref, go_here, loc.at[0])
    own_go.start()
    go_in = [remote(go_ref, go_here, gos_ss.at[0], gos_rs.at[0], sibling)]
    w_in = remote(
        w_ref.at[pl.ds((1 - core) * half, half)], w_v.at[core], w_ss.at[0], w_rs.at[0], sibling
    )
    own_w = pltpu.make_async_copy(w_ref.at[pl.ds(core * half, half)], w_v.at[core], loc.at[1])
    own_w.start()
    for k in range(2):
        for d in range(2):
            push(me, d, k, 0, hid_v.at[pl.ds((2 * d + k) * quarter, quarter)])
    own_hid = pltpu.make_async_copy(hid_v, hid_ref.at[me], loc.at[2])
    own_hid.start()

    def arrived(step, d, k):
        ag_in[d, k].wait_recv()
        origin = (place + n - step - 1) % n if d == 0 else (place + step + 1) % n
        src_row = row_of(origin)
        if step < n - 2:
            block = hid_ref.at[src_row, pl.ds((2 * d + k) * quarter, quarter)]
            ag_in[d, k] = remote(
                block, block, ag_ss.at[d, k, step + 1], ag_rs.at[d, k, step + 1], towards[d]
            )
        push(src_row, d, k, step + 1)

    for step in range(n - 2):
        for k in range(2):
            for d in range(2):
                arrived(step, d, k)

    for step in range(n_col - 1):
        z_in[step].wait_recv()
        block = go_v.at[core, pl.ds((z + n_col - step - 1) % n_col * rows, rows)]
        go_in.append(remote(block, block, gos_ss.at[step + 1], gos_rs.at[step + 1], sibling))
    own_go.wait()
    out_go = pltpu.make_async_copy(go_v.at[core], gath_ref, loc.at[3])
    out_go.start()
    for copy in go_in:
        copy.wait_recv()
    w_in.wait_recv()
    own_w.wait()

    def partial_of(ring_place, d):
        base = pl.multiple_of(snake(ring_place) * (2 * tok), 2 * tok)

        @pl.loop(0, quarter // tile)
        def _(j):
            columns = pl.ds(pl.multiple_of(d * quarter + j * tile, 128), tile)
            total = None
            for c in range(2):
                term = lax.dot_general(
                    go_v[c, pl.ds(base, 2 * tok), :], w_v[c, columns, :],
                    (((1,), (1,)), ((), ())), preferred_element_type=F32,
                )
                total = term if total is None else total + term
            part[d, :, pl.ds(pl.multiple_of(j * tile, 128), tile)] = total

    offsets = (pl.multiple_of((1 - core) * tok, tok), pl.multiple_of(core * tok, tok))
    last_refs = ((last_ref0, last_ref1), (last_ref2, last_ref3))
    rs_hop, fin, last = {}, [], []

    def own_partials():
        for d in range(2):
            partial_of(place, d)
        for d in range(2):

            @pl.loop(0, quarter // tile)
            def _(j):
                span = pl.ds(pl.multiple_of(j * tile, 128), tile)
                sib_out[d, :, span] = part[d, pl.ds(offsets[0], tok), span].astype(BF16)
                columns = pl.ds(pl.multiple_of(core * half + d * quarter + j * tile, 128), tile)
                own_v[:, columns] = part[d, pl.ds(offsets[1], tok), span]

            fin.append(remote(sib_out.at[d], sib_in.at[d], fin_ss.at[d], fin_rs.at[d], sibling))

    for step in range(n - 1):
        for d in range(2):
            partial_of((place + n - 1 - step) % n if d == 0 else (place + 1 + step) % n, d)
        for k in range(2):
            for d in range(2):
                if step > 0:
                    rs_hop[d, k].wait_recv()

                @pl.loop(0, quarter // tile)
                def _(j):
                    span = pl.ds(pl.multiple_of(j * tile, 128), tile)
                    value = part[d, pl.ds(offsets[k], tok), span]
                    if step > 0:
                        value = value + rs_in[d, k, step - 1, :, span].astype(F32)
                    rs_out[d, k, step, :, span] = value.astype(BF16)

                if step < n - 2:
                    rs_hop[d, k] = remote(
                        rs_out.at[d, k, step], rs_in.at[d, k, step],
                        rs_ss.at[d, k, step], rs_rs.at[d, k, step], towards[d],
                    )
                else:
                    copy = pltpu.make_async_copy(
                        rs_out.at[d, k, step], last_refs[d][k], last_sem.at[d, k]
                    )
                    copy.start()
                    last.append(copy)
        if step == 0:
            for k in range(2):
                for d in range(2):
                    arrived(n - 2, d, k)
        if step == n - 3:
            own_partials()
            for d in range(2):
                fin[d].wait_recv()

                @pl.loop(0, quarter // tile)
                def _(j):
                    span = pl.ds(pl.multiple_of(j * tile, 128), tile)
                    columns = pl.ds(
                        pl.multiple_of((1 - core) * half + d * quarter + j * tile, 128), tile
                    )
                    own_v[:, columns] = sib_in[d, :, span].astype(F32)

            own_out = pltpu.make_async_copy(own_v, own_ref, loc.at[0])
            own_out.start()

    own_out.wait()
    for copy in last:
        copy.wait()
    for copy in push_in:
        copy.wait_recv()
    for copy in sent:
        copy.wait_send()
    own_hid.wait()
    out_go.wait()


def exchange(n_row, n_col, gate, up, go, w):
    tok, ff = gate.shape
    rows, width = go.shape
    n = n_row // 2
    quarter = ff // 4
    dma = pltpu.SemaphoreType.DMA
    whole = pl.BlockSpec(memory_space=pltpu.VMEM)
    hbm = pl.BlockSpec(memory_space=pl.ANY)
    return pl.pallas_call(
        functools.partial(exchange_kernel, n_row, n_col),
        out_shape=(
            jax.ShapeDtypeStruct((n_row, ff, tok), BF16),
            jax.ShapeDtypeStruct((n_col * rows, width), BF16),
            jax.ShapeDtypeStruct((tok, ff), F32),
        )
        + (jax.ShapeDtypeStruct((tok, quarter), BF16),) * 4,
        in_specs=[whole, whole, hbm, hbm],
        out_specs=(hbm,) * 7,
        scratch_shapes=[
            pltpu.VMEM((ff, tok), BF16),
            pltpu.VMEM((2, ff // 2, width), BF16),
            pltpu.VMEM((2, n_col * rows, width), BF16),
            pltpu.VMEM((2, 2 * tok, quarter), F32),
            pltpu.VMEM((tok, ff), F32),
            pltpu.VMEM((2, 2, n - 1, tok, quarter), BF16),
            pltpu.VMEM((2, 2, n - 2, tok, quarter), BF16),
            pltpu.VMEM((2, tok, quarter), BF16),
            pltpu.VMEM((2, tok, quarter), BF16),
            dma((2, 2, n - 1)),
            dma((2, 2, n - 1)),
            dma((2, 2, n)),
            dma((2, 2, n)),
            dma((n_col - 1,)),
            dma((n_col - 1,)),
            dma((n_col,)),
            dma((n_col,)),
            dma((1,)),
            dma((1,)),
            dma((2, 2, n - 2)),
            dma((2, 2, n - 2)),
            dma((2,)),
            dma((2,)),
            dma((4,)),
            dma((2, 2)),
        ],
        compiler_params=pltpu.CompilerParams(
            collective_id=0, has_side_effects=True, vmem_limit_bytes=56 * 2**20
        ),
    )(gate, up, go, w)


def weight_kernel(n_row, hid_ref, go_ref, gw_ref):
    lhs = jnp.concatenate([hid_ref[r] for r in range(n_row)], axis=1)
    gw_ref[...] = jnp.dot(lhs, go_ref[...], preferred_element_type=F32)


def weight_gradient(hid, go):
    n_row, ff, tok = hid.shape
    tokens, width = go.shape
    tile = 512 if ff % 512 == 0 else 256
    return pl.pallas_call(
        functools.partial(weight_kernel, n_row),
        grid=(ff // tile,),
        out_shape=jax.ShapeDtypeStruct((ff, width), F32),
        in_specs=[
            pl.BlockSpec((n_row, tile, tok), lambda j: (0, j, 0)),
            pl.BlockSpec((tokens, width), lambda j: (0, 0)),
        ],
        out_specs=pl.BlockSpec((tile, width), lambda j: (j, 0)),
        cost_estimate=pl.CostEstimate(
            flops=2 * ff * tokens * width,
            bytes_accessed=2 * ff * tokens + 2 * tokens * width + 4 * ff * width,
            transcendentals=0,
        ),
        compiler_params=pltpu.CompilerParams(vmem_limit_bytes=58 * 2**20),
    )(hid, go)


def activation_kernel(core_ref, r0, r1, r2, r3, own_ref, gate_ref, up_ref, gg_ref, gu_ref):
    step = pl.program_id(0)
    for index, sums in enumerate((r0, r1, r2, r3)):

        @pl.when(step == index)
        def _():
            gate = gate_ref[...].astype(F32)
            grad_hidden = own_ref[...] + sums[0].astype(F32)
            sigma = jax.nn.sigmoid(gate)
            gu_ref[...] = (grad_hidden * (gate * sigma)).astype(BF16)
            gg_ref[...] = (
                grad_hidden * up_ref[...].astype(F32) * sigma * (1.0 + gate * (1.0 - sigma))
            ).astype(BF16)


def activation_pass(core, sums, own, gate, up):
    tok, ff = gate.shape
    quarter = ff // 4

    def strip_at(step, core_ref):
        k, d = step // 2, step % 2
        owner = k * core_ref[0] + (1 - k) * (1 - core_ref[0])
        return (0, owner * 2 + d)

    strip = pl.BlockSpec((tok, quarter), strip_at)
    whole = pl.BlockSpec((1, tok, quarter), lambda step, core_ref: (0, 0, 0))
    return pl.pallas_call(
        activation_kernel,
        out_shape=(jax.ShapeDtypeStruct((tok, ff), BF16),) * 2,
        grid_spec=pltpu.PrefetchScalarGridSpec(
            num_scalar_prefetch=1,
            grid=(4,),
            in_specs=[whole] * 4 + [strip] * 3,
            out_specs=(strip, strip),
        ),
        compiler_params=pltpu.CompilerParams(vmem_limit_bytes=58 * 2**20),
    )(core, *[s[None] for s in sums], own, gate, up)


def solution(mesh):
    n_row, n_col = mesh.shape["row"], mesh.shape["col"]
    n = n_row // 2

    def last_hop(value, d, k):
        move = 1 if d == 0 else n - 1
        pairs = [
            (snake(p) * 2 + c, snake((p + move) % n) * 2 + (c if k == 1 else 1 - c))
            for p in range(n)
            for c in range(2)
        ]
        return lax.ppermute(value, "row", pairs)

    def body(gate_input, up_input, grad_output, down_weight):
        hid, go, own, *last = exchange(n_row, n_col, gate_input, up_input, grad_output, down_weight)
        sums = [last_hop(last[2 * d + k], d, k) for k in range(2) for d in range(2)]
        grad_weight = weight_gradient(hid, go)
        core = (lax.axis_index("row") % 2).astype(jnp.int32).reshape(1)
        grad_gate, grad_up = activation_pass(core, sums, own, gate_input, up_input)
        return grad_gate, grad_up, grad_weight

    placed = (P("row", "col"), P("row", "col"), P("col", "row"), P("col", "row"))
    return jax.shard_map(
        body,
        mesh=mesh,
        in_specs=placed,
        out_specs=(P("row", "col"), P("row", "col"), P("col", "row")),
        check_vma=False,
    )
```

```python
import functools

import jax
import jax.numpy as jnp
from jax import lax
from jax.experimental import pallas as pl
from jax.experimental.pallas import tpu as pltpu
from jax.sharding import PartitionSpec as P

F32 = jnp.float32
BF16 = jnp.bfloat16
MESH = pl.DeviceIdType.MESH


def snake(place):
    return (place // 2) * 2 + (place + place // 2) % 2


def tile_of(width):
    return 256 if width % 256 == 0 else 128


def exchange_kernel(
    n_row, n_col, gate_ref, up_ref, go_ref, w_ref,
    hid_ref, gath_ref, own_ref, last_ref0, last_ref1, last_ref2, last_ref3,
    hid_v, w_v, go_v, part, own_v, rs_out, rs_in, sib_out, sib_in,
    ag_ss, ag_rs, push_ss, push_rs, z_ss, z_rs, gos_ss, gos_rs, w_ss, w_rs, rs_ss, rs_rs,
    fin_ss, fin_rs, loc, last_sem,
):
    me, z = lax.axis_index("row"), lax.axis_index("col")
    core, chip = me % 2, me // 2
    n = n_row // 2
    place = snake(chip)
    tok, ff = gate_ref.shape
    rows = go_ref.shape[0]
    half, quarter = ff // 2, ff // 4
    tile = tile_of(quarter)

    def row_of(ring_place):
        return snake(ring_place) * 2 + core

    sibling = (chip * 2 + 1 - core, z)
    ahead = (row_of((place + 1) % n), z)
    behind = (row_of((place + n - 1) % n), z)
    towards = (ahead, behind)
    z_peers = [(me, (z + step) % n_col) for step in range(1, n_col)]

    barrier = pltpu.get_barrier_semaphore()
    for peer in [ahead, behind, sibling] + z_peers:
        pl.semaphore_signal(barrier, inc=1, device_id=peer, device_id_type=MESH)
    pl.semaphore_wait(barrier, 3 + len(z_peers))

    sent = []

    def remote(src, dst, ss, rs, peer):
        copy = pltpu.make_async_remote_copy(
            src_ref=src, dst_ref=dst, send_sem=ss, recv_sem=rs, device_id=peer, device_id_type=MESH
        )
        copy.start()
        sent.append(copy)
        return copy

    go_here = go_v.at[core, pl.ds(z * rows, rows)]
    z_in = []
    for step, peer in enumerate(z_peers):
        z_in.append(remote(go_ref, go_here, z_ss.at[step], z_rs.at[step], peer))

    ag_in, push_in = {}, []

    def push(src_row, d, k, slot, src=None):
        span = pl.ds((2 * d + k) * quarter, quarter)
        dst = hid_ref.at[src_row, span]
        push_in.append(
            remote(dst if src is None else src, dst, push_ss.at[d, k, slot], push_rs.at[d, k, slot], sibling)
        )

    def hidden_quarter(d, k):
        first = (2 * d + k) * quarter

        @pl.loop(0, quarter // tile)
        def _(j):
            span = pl.ds(pl.multiple_of(first + j * tile, 128), tile)
            gate = gate_ref[:, span].astype(F32)
            value = gate * jax.nn.sigmoid(gate) * up_ref[:, span].astype(F32)
            hid_v[span, :] = value.T.astype(BF16)

    def first_hop(d, k):
        span = pl.ds((2 * d + k) * quarter, quarter)
        ag_in[d, k] = remote(
            hid_v.at[span], hid_ref.at[me, span], ag_ss.at[d, k, 0], ag_rs.at[d, k, 0], towards[d]
        )

    for d in range(2):
        hidden_quarter(d, 0)
        first_hop(d, 0)
    for d in range(2):
        hidden_quarter(d, 1)

    own_go = pltpu.make_async_copy(go_ref, go_here, loc.at[0])
    own_go.start()
    go_in = [remote(go_ref, go_here, gos_ss.at[0], gos_rs.at[0], sibling)]
    w_in = remote(
        w_ref.at[pl.ds((1 - core) * half, half)], w_v.at[core], w_ss.at[0], w_rs.at[0], sibling
    )
    own_w = pltpu.make_async_copy(w_ref.at[pl.ds(core * half, half)], w_v.at[core], loc.at[1])
    own_w.start()
    for k in range(2):
        for d in range(2):
            push(me, d, k, 0, hid_v.at[pl.ds((2 * d + k) * quarter, quarter)])
    own_hid = pltpu.make_async_copy(hid_v, hid_ref.at[me], loc.at[2])
    own_hid.start()
    for d in range(2):
        ag_in[d, 0].wait_send()
        sent[:] = [copy for copy in sent if copy is not ag_in[d, 0]]
        first_hop(d, 1)

    def arrived(step, d, k):
        ag_in[d, k].wait_recv()
        origin = (place + n - step - 1) % n if d == 0 else (place + step + 1) % n
        src_row = row_of(origin)
        if step < n - 2:
            block = hid_ref.at[src_row, pl.ds((2 * d + k) * quarter, quarter)]
            ag_in[d, k] = remote(
                block, block, ag_ss.at[d, k, step + 1], ag_rs.at[d, k, step + 1], towards[d]
            )
        push(src_row, d, k, step + 1)

    for step in range(n - 2):
        for k in range(2):
            for d in range(2):
                arrived(step, d, k)

    for step in range(n_col - 1):
        z_in[step].wait_recv()
        block = go_v.at[core, pl.ds((z + n_col - step - 1) % n_col * rows, rows)]
        go_in.append(remote(block, block, gos_ss.at[step + 1], gos_rs.at[step + 1], sibling))
    own_go.wait()
    out_go = pltpu.make_async_copy(go_v.at[core], gath_ref, loc.at[3])
    out_go.start()
    for copy in go_in:
        copy.wait_recv()
    w_in.wait_recv()
    own_w.wait()

    def partial_of(ring_place, d):
        base = pl.multiple_of(snake(ring_place) * (2 * tok), 2 * tok)

        @pl.loop(0, quarter // tile)
        def _(j):
            columns = pl.ds(pl.multiple_of(d * quarter + j * tile, 128), tile)
            total = None
            for c in range(2):
                term = lax.dot_general(
                    go_v[c, pl.ds(base, 2 * tok), :], w_v[c, columns, :],
                    (((1,), (1,)), ((), ())), preferred_element_type=F32,
                )
                total = term if total is None else total + term
            part[d, :, pl.ds(pl.multiple_of(j * tile, 128), tile)] = total

    offsets = (pl.multiple_of((1 - core) * tok, tok), pl.multiple_of(core * tok, tok))
    last_refs = ((last_ref0, last_ref1), (last_ref2, last_ref3))
    rs_hop, fin, last = {}, [], []

    def own_partials():
        for d in range(2):
            partial_of(place, d)
        for d in range(2):

            @pl.loop(0, quarter // tile)
            def _(j):
                span = pl.ds(pl.multiple_of(j * tile, 128), tile)
                sib_out[d, :, span] = part[d, pl.ds(offsets[0], tok), span].astype(BF16)
                columns = pl.ds(pl.multiple_of(core * half + d * quarter + j * tile, 128), tile)
                own_v[:, columns] = part[d, pl.ds(offsets[1], tok), span]

            fin.append(remote(sib_out.at[d], sib_in.at[d], fin_ss.at[d], fin_rs.at[d], sibling))

    def round_out(step, d, k):
        if step > 0:
            rs_hop[d, k].wait_recv()

        @pl.loop(0, quarter // tile)
        def _(j):
            span = pl.ds(pl.multiple_of(j * tile, 128), tile)
            value = part[d, pl.ds(offsets[k], tok), span]
            if step > 0:
                value = value + rs_in[d, k, step - 1, :, span].astype(F32)
            rs_out[d, k, step, :, span] = value.astype(BF16)

    def send_out(step, d, k):
        if step < n - 2:
            rs_hop[d, k] = remote(
                rs_out.at[d, k, step], rs_in.at[d, k, step],
                rs_ss.at[d, k, step], rs_rs.at[d, k, step], towards[d],
            )
        else:
            copy = pltpu.make_async_copy(rs_out.at[d, k, step], last_refs[d][k], last_sem.at[d, k])
            copy.start()
            last.append(copy)

    def partial_at(step, d):
        partial_of((place + n - 1 - step) % n if d == 0 else (place + 1 + step) % n, d)

    for d in range(2):
        partial_at(0, d)
        round_out(0, d, 0)
        send_out(0, d, 0)
        round_out(0, d, 1)
    for step in range(n - 1):
        if step == 0:
            partial_at(1, 0)
            for d in range(2):
                send_out(0, d, 1)
            partial_at(1, 1)
        else:
            if step > 1:
                for d in range(2):
                    partial_at(step, d)
            for k in range(2):
                for d in range(2):
                    round_out(step, d, k)
                    send_out(step, d, k)
        if step == 1:
            for k in range(2):
                for d in range(2):
                    arrived(n - 2, d, k)
        if step == n - 3:
            own_partials()
            for d in range(2):
                fin[d].wait_recv()

                @pl.loop(0, quarter // tile)
                def _(j):
                    span = pl.ds(pl.multiple_of(j * tile, 128), tile)
                    columns = pl.ds(
                        pl.multiple_of((1 - core) * half + d * quarter + j * tile, 128), tile
                    )
                    own_v[:, columns] = sib_in[d, :, span].astype(F32)

            own_out = pltpu.make_async_copy(own_v, own_ref, loc.at[0])
            own_out.start()

    own_out.wait()
    for copy in last:
        copy.wait()
    for copy in push_in:
        copy.wait_recv()
    for copy in sent:
        copy.wait_send()
    own_hid.wait()
    out_go.wait()


def exchange(n_row, n_col, gate, up, go, w):
    tok, ff = gate.shape
    rows, width = go.shape
    n = n_row // 2
    quarter = ff // 4
    dma = pltpu.SemaphoreType.DMA
    whole = pl.BlockSpec(memory_space=pltpu.VMEM)
    hbm = pl.BlockSpec(memory_space=pl.ANY)
    return pl.pallas_call(
        functools.partial(exchange_kernel, n_row, n_col),
        out_shape=(
            jax.ShapeDtypeStruct((n_row, ff, tok), BF16),
            jax.ShapeDtypeStruct((n_col * rows, width), BF16),
            jax.ShapeDtypeStruct((tok, ff), F32),
        )
        + (jax.ShapeDtypeStruct((tok, quarter), BF16),) * 4,
        in_specs=[whole, whole, hbm, hbm],
        out_specs=(hbm,) * 7,
        scratch_shapes=[
            pltpu.VMEM((ff, tok), BF16),
            pltpu.VMEM((2, ff // 2, width), BF16),
            pltpu.VMEM((2, n_col * rows, width), BF16),
            pltpu.VMEM((2, 2 * tok, quarter), F32),
            pltpu.VMEM((tok, ff), F32),
            pltpu.VMEM((2, 2, n - 1, tok, quarter), BF16),
            pltpu.VMEM((2, 2, n - 2, tok, quarter), BF16),
            pltpu.VMEM((2, tok, quarter), BF16),
            pltpu.VMEM((2, tok, quarter), BF16),
            dma((2, 2, n - 1)),
            dma((2, 2, n - 1)),
            dma((2, 2, n)),
            dma((2, 2, n)),
            dma((n_col - 1,)),
            dma((n_col - 1,)),
            dma((n_col,)),
            dma((n_col,)),
            dma((1,)),
            dma((1,)),
            dma((2, 2, n - 2)),
            dma((2, 2, n - 2)),
            dma((2,)),
            dma((2,)),
            dma((4,)),
            dma((2, 2)),
        ],
        compiler_params=pltpu.CompilerParams(
            collective_id=0, has_side_effects=True, vmem_limit_bytes=56 * 2**20
        ),
    )(gate, up, go, w)


def weight_kernel(n_row, hid_ref, go_ref, gw_ref):
    lhs = jnp.concatenate([hid_ref[r] for r in range(n_row)], axis=1)
    gw_ref[...] = jnp.dot(lhs, go_ref[...], preferred_element_type=F32)


def weight_gradient(hid, go):
    n_row, ff, tok = hid.shape
    tokens, width = go.shape
    tile = next(t for t in (1792, 1024, 512, 256) if ff % t == 0)
    return pl.pallas_call(
        functools.partial(weight_kernel, n_row),
        grid=(ff // tile,),
        out_shape=jax.ShapeDtypeStruct((ff, width), F32),
        in_specs=[
            pl.BlockSpec((n_row, tile, tok), lambda j: (0, j, 0)),
            pl.BlockSpec((tokens, width), lambda j: (0, 0)),
        ],
        out_specs=pl.BlockSpec((tile, width), lambda j: (j, 0)),
        cost_estimate=pl.CostEstimate(
            flops=2 * ff * tokens * width,
            bytes_accessed=2 * ff * tokens + 2 * tokens * width + 4 * ff * width,
            transcendentals=0,
        ),
        compiler_params=pltpu.CompilerParams(vmem_limit_bytes=50 * 2**20),
    )(hid, go)


def activation_kernel(core_ref, r0, r1, r2, r3, own_ref, gate_ref, up_ref, gg_ref, gu_ref):
    step = pl.program_id(0)
    for index, sums in enumerate((r0, r1, r2, r3)):

        @pl.when(step == index)
        def _():
            gate = gate_ref[...].astype(F32)
            grad_hidden = own_ref[...] + sums[0].astype(F32)
            sigma = jax.nn.sigmoid(gate)
            gu_ref[...] = (grad_hidden * (gate * sigma)).astype(BF16)
            gg_ref[...] = (
                grad_hidden * up_ref[...].astype(F32) * sigma * (1.0 + gate * (1.0 - sigma))
            ).astype(BF16)


def activation_pass(core, sums, own, gate, up):
    tok, ff = gate.shape
    quarter = ff // 4

    def strip_at(step, core_ref):
        k, d = step // 2, step % 2
        owner = k * core_ref[0] + (1 - k) * (1 - core_ref[0])
        return (0, owner * 2 + d)

    strip = pl.BlockSpec((tok, quarter), strip_at)
    whole = pl.BlockSpec((1, tok, quarter), lambda step, core_ref: (0, 0, 0))
    return pl.pallas_call(
        activation_kernel,
        out_shape=(jax.ShapeDtypeStruct((tok, ff), BF16),) * 2,
        grid_spec=pltpu.PrefetchScalarGridSpec(
            num_scalar_prefetch=1,
            grid=(4,),
            in_specs=[whole] * 4 + [strip] * 3,
            out_specs=(strip, strip),
        ),
        compiler_params=pltpu.CompilerParams(vmem_limit_bytes=48 * 2**20),
    )(core, *[s[None] for s in sums], own, gate, up)


def solution(mesh):
    n_row, n_col = mesh.shape["row"], mesh.shape["col"]
    n = n_row // 2

    def last_hop(value, d, k):
        move = 1 if d == 0 else n - 1
        pairs = [
            (snake(p) * 2 + c, snake((p + move) % n) * 2 + (c if k == 1 else 1 - c))
            for p in range(n)
            for c in range(2)
        ]
        return lax.ppermute(value, "row", pairs)

    def body(gate_input, up_input, grad_output, down_weight):
        hid, go, own, *last = exchange(n_row, n_col, gate_input, up_input, grad_output, down_weight)
        sums = [last_hop(last[2 * d + k], d, k) for k in range(2) for d in range(2)]
        grad_weight = weight_gradient(hid, go)
        core = (lax.axis_index("row") % 2).astype(jnp.int32).reshape(1)
        grad_gate, grad_up = activation_pass(core, sums, own, gate_input, up_input)
        return grad_gate, grad_up, grad_weight

    placed = (P("row", "col"), P("row", "col"), P("col", "row"), P("col", "row"))
    return jax.shard_map(
        body,
        mesh=mesh,
        in_specs=placed,
        out_specs=(P("row", "col"), P("row", "col"), P("col", "row")),
        check_vma=False,
    )
```
